1024 devices in a mesh: dp: 16 (over x, core), expert: 64 (over y, z).
Axes of the slice: x: 8, y: 8, z: 8, core: 2. Of those that a mesh axis runs over, the one named last changes fastest.
Arguments:
- preactivations: bfloat16 [16384, 8, 1536], P(('dp', 'expert')), may hold values from -6 to 6
- route_weights: float32 [16384, 8], P(('dp', 'expert')), may hold values from 0.05 to 0.3
- expert_ids: int32 [16384, 8], P(('dp', 'expert')), may hold values from 0 to 63, all different within a row; in each aligned block of 16 rows (0 to 15, 16 to 31, ...) at most 4 rows name the same one
- down_proj: bfloat16 [64, 4096, 768], P('expert'), may hold values from -0.21875 to 0.21875
- output_cotangent: bfloat16 [16384, 4096], P(('dp', 'expert')), may hold values from -6 to 6
Outputs:
- mixed: bfloat16 [16384, 4096], P(('dp', 'expert'))
- route_grads: float32 [16384, 8], P(('dp', 'expert'))
- pre_grads: bfloat16 [16384, 8, 1536], P(('dp', 'expert'))
- down_grads: float32 [64, 4096, 768], P('expert', 'dp')
The draws below stay inside these ranges and needn't reach their ends.
Inputs may be any that keep to these rules, and one draw needn't show every extreme that they name: `expert_ids`: among the 128 slots of one device's tokens, no expert is named more than 4 times, a bound that some block reaches; a token's 8 experts are distinct.
All inputs are finite; a program needn't handle non-finite values.
Results may differ from the reference program's by a relative error of at most 0.017.
Values may be sent and summed in bfloat16 or wider, within the bound.
No kernel may reach another device: no remote copies, remote signals or barrier semaphores. Data moves between devices by JAX's collectives and lax.ppermute only.
A program may use at most 64 MiB of HBM per device.

```python
import math
import jax
import jax.numpy as jnp
import numpy as np
from jax import lax

D = 4096
TOP = 8
HID = 768
TOK_DEV = 16
EXPERTS = 64
CAP = 4
TOKENS = 16384
N_DP = 16
N_EXPERT = 64


def spiked(result, stream_key, source, target, parts, factor):
    def block_of(axis_at):
        return (jnp.arange(result.shape[axis_at]) // (result.shape[axis_at] // parts)).reshape((-1,) + (1,) * (result.ndim - 1 - axis_at))

    near = jax.random.permutation(stream_key, parts)[block_of(target)]
    far = (block_of(target) + parts // 2) % parts
    return jnp.where((block_of(source) == near) | (block_of(source) == far), factor * result, result)


def block_levels(stream_key, dims, pieces, smallest, high):
    factor_of, own = 1.0, jax.random.fold_in(stream_key, 6)
    for dim, blocks in pieces:
        heights = jnp.exp(jax.random.uniform(jax.random.fold_in(own, dim), (blocks,), jnp.float32, smallest / len(pieces), high / len(pieces)))
        factor_of = factor_of * jnp.repeat(heights, dims[dim] // blocks).reshape([-1 if axis == dim else 1 for axis in range(len(dims))])
    return factor_of


def deal_out(key, own, number, rows, amount, top, most, slope):
    order = jax.random.permutation(key, amount)
    crowded, usual = load_shares(amount, rows * top, most, slope, True), load_shares(amount, rows * top, most, slope, False)
    places = jnp.arange(amount)

    def named(sizes, offset_by):
        used = int((sizes > 0).sum())
        fixed = max(1, used // 4)
        passed = fixed + (places - fixed + offset_by * (used - fixed)) % max(1, amount - fixed)
        return jnp.zeros((amount,), jnp.int32).at[order[jnp.where(places < fixed, places, passed)]].set(jnp.asarray(sizes, jnp.int32))

    sizes = jnp.where(number % 4 == 0, named(crowded, number // 4), named(usual, number - number // 4 - 1))
    mixed = jax.random.permutation(jax.random.fold_in(own, 3), amount)
    source_of, receiver = mixed[0:amount // 2 * 2:2], mixed[1:amount // 2 * 2:2]
    slack = jnp.minimum(sizes[source_of] - 1, most - sizes[receiver]) // 2
    slack = jnp.where((source_of == order[0]) | (receiver == order[0]) | (sizes[receiver] == 0), 0, jnp.maximum(slack, 0))
    passed = jax.random.randint(jax.random.fold_in(own, 4), (amount // 2,), 0, 1 << 20) % (slack + 1)
    sizes = sizes.at[source_of].add(-passed).at[receiver].add(passed)
    labels = jnp.searchsorted(jnp.cumsum(sizes), jnp.arange(rows * top), side="right").astype(jnp.int32)
    listing = labels.reshape(top, rows).T
    listing = listing[jax.random.permutation(jax.random.fold_in(own, 1), rows)]
    offset_by = jax.random.randint(jax.random.fold_in(own, 2), (rows, 1), 0, top)
    return jnp.take_along_axis(listing, (jnp.arange(top)[None, :] + offset_by) % top, axis=1)


def load_shares(count, total, reach, slope, full):
    loads = [(1 << 20) // math.isqrt(grade ** slope) + 1 for grade in range(1, count + 1)]
    largest = reach if full else min(reach, max(-(-total // count), total * loads[0] // sum(loads)))
    least = 1 if total - largest >= count - 1 else 0
    given, spare = [largest] + [least] * (count - 1), total - largest - least * (count - 1)
    while spare > 0:
        free = [i for i in range(1, count) if given[i] < largest] or [i for i in range(1, count) if given[i] < reach]
        mass, budget = sum([loads[i] for i in free]), spare
        for i in free:
            addition = min(reach - given[i], max(1, budget * loads[i] // mass), spare)
            given[i] = given[i] + addition
            spare = spare - addition
    return np.array(given)


def scatter_about(rng, dims, spread, reach, split=(), kind=jnp.bfloat16):
    loudness = block_levels(rng, dims, split, -0.22, 0.18) if split else 1.0
    drawn = jax.random.normal(rng, dims, jnp.float32) * spread * loudness
    return jnp.minimum(jnp.maximum(drawn, -reach), reach).astype(kind)


def heavy_noise(own_key, shape, width, most, cuts, heavy, kind=jnp.bfloat16):
    array = width * jax.random.normal(own_key, shape, jnp.float32)
    if cuts:
        array = array * block_levels(own_key, shape, cuts, -0.22, 0.18)
    return jnp.clip(spiked(array, jax.random.fold_in(own_key, 3), *heavy), -most, most).astype(kind)


def setup_inputs(seed: int = 0) -> dict:
    keys = jax.random.split(jax.random.key(seed), 6)
    preactivations = scatter_about(keys[0], (TOKENS, TOP, 2 * HID), 1.0, 6.0, ((0, 1024),))
    route_weights = jnp.clip(0.05 + 0.25 * jax.random.uniform(keys[1], (TOKENS, TOP), jnp.float32) ** block_levels(keys[1], (TOKENS, TOP), ((0, 1024),), -0.2, 0.2), 0.05, 0.3)
    expert_ids_keys = jax.random.split(jax.random.fold_in(keys[2], 1), TOKENS // TOK_DEV)
    expert_ids_turns = jax.random.permutation(jax.random.fold_in(keys[2], 3), TOKENS // TOK_DEV)
    expert_ids = jax.vmap(lambda own, number: deal_out(jax.random.fold_in(keys[2], 2), own, number, TOK_DEV, EXPERTS, TOP, CAP, 2))(expert_ids_keys, expert_ids_turns).reshape((TOKENS, TOP))
    down_proj = scatter_about(keys[3], (EXPERTS, D, HID), HID ** -0.5, 0.21875, ((0, 64),))
    output_cotangent = heavy_noise(keys[4], (TOKENS, D), 0.25, 6.0, ((0, 1024),), (0, 1, 1024, 6.0))
    return dict(preactivations=preactivations, route_weights=route_weights, expert_ids=expert_ids, down_proj=down_proj, output_cotangent=output_cotangent)


def rounded(values):
    return lax.optimization_barrier(values.astype(jnp.bfloat16)).astype(jnp.float32)


def reference(preactivations, route_weights, expert_ids, down_proj, output_cotangent):
    weight = down_proj.astype(jnp.float32)
    slot_count = TOK_DEV * TOP
    pre_all = preactivations.reshape(N_DP, N_EXPERT, slot_count, 2 * HID)
    route_all = route_weights.reshape(N_DP, N_EXPERT, TOK_DEV, TOP)
    ids_all = expert_ids.reshape(N_DP, N_EXPERT, slot_count)
    cot_all = output_cotangent.reshape(N_DP, N_EXPERT, TOK_DEV, D)
    source = jnp.broadcast_to(jnp.arange(N_EXPERT, dtype=jnp.int32)[:, None], (N_EXPERT, slot_count))

    def one_row(running, row_block):
        pre_blk, route_blk, ids_blk, cot_blk = row_block
        pre_vals = pre_blk.astype(jnp.float32)
        gate_pre = pre_vals[..., :HID]
        up_pre = pre_vals[..., HID:]
        sigmoid_gate = jax.nn.sigmoid(gate_pre)
        activated = gate_pre * sigmoid_gate
        hidden = rounded(activated * up_pre)
        cotangent = cot_blk.astype(jnp.float32)
        scaled = rounded(route_blk[..., None] * cotangent[:, :, None, :]).reshape(N_EXPERT, slot_count, D)
        onehot = (ids_blk[..., None] == jnp.arange(EXPERTS, dtype=jnp.int32)).astype(jnp.int32)
        earlier = (jnp.cumsum(onehot, axis=1).astype(jnp.int32) - onehot) * onehot
        slot_rank = jnp.sum(earlier, axis=-1).astype(jnp.int32)
        hidden_buf = jnp.zeros((EXPERTS, N_EXPERT, CAP, HID), jnp.float32).at[ids_blk, source, slot_rank].set(hidden)
        cot_buf = jnp.zeros((EXPERTS, N_EXPERT, CAP, D), jnp.float32).at[ids_blk, source, slot_rank].set(scaled)
        out_buf = rounded(jnp.einsum("escf,edf->escd", hidden_buf, weight))
        grad_buf = rounded(jnp.einsum("escd,edf->escf", cot_buf, weight))
        part_sum = rounded(jnp.einsum("escf,escd->edf", hidden_buf, cot_buf))
        slot_outs = out_buf[ids_blk, source, slot_rank].reshape(N_EXPERT, TOK_DEV, TOP, D)
        slot_grad = grad_buf[ids_blk, source, slot_rank]
        mixed = jnp.einsum("jtk,jtkd->jtd", route_blk, slot_outs).astype(jnp.bfloat16)
        route_grads = jnp.einsum("jtkd,jtd->jtk", slot_outs, cotangent)
        gate_grad = slot_grad * up_pre * (sigmoid_gate * (1.0 + gate_pre * (1.0 - sigmoid_gate)))
        up_grad = slot_grad * activated
        pre_grads = jnp.concatenate([gate_grad, up_grad], axis=-1).astype(jnp.bfloat16)
        return running + part_sum, (mixed, route_grads, pre_grads)

    start_grads = jnp.zeros((EXPERTS, D, HID), jnp.float32)
    down_grads, outputs = lax.scan(one_row, start_grads, (pre_all, route_all, ids_all, cot_all))
    mixed, route_grads, pre_grads = outputs
    mixed = mixed.reshape(TOKENS, D)
    route_grads = route_grads.reshape(TOKENS, TOP)
    pre_grads = pre_grads.reshape(TOKENS, TOP, 2 * HID)
    return mixed, route_grads, pre_grads, down_grads
```

```python
import functools

import jax
import jax.numpy as jnp
from jax import lax
from jax.experimental import pallas as pl
from jax.experimental.pallas import tpu as pltpu
from jax.sharding import Mesh, PartitionSpec as P


F32 = jnp.float32
BF16 = jnp.bfloat16
CAP = 4


def iota(shape, dim):
    return lax.broadcasted_iota(jnp.int32, shape, dim)


def mm(a, b, dims=((1,), (0,))):
    return lax.dot_general(a, b, (dims, ((), ())), preferred_element_type=F32)


def by_slot(values_t, tokens):
    return jnp.concatenate(
        [jnp.broadcast_to(values_t[:, t : t + 1], (values_t.shape[0], 128)) for t in range(tokens)],
        axis=0,
    )


def gate_terms(pre_ref, hid):
    gate = pre_ref[:, :hid].astype(F32)
    up = pre_ref[:, hid:].astype(F32)
    sig = jax.nn.sigmoid(gate)
    return gate, up, sig


def prep_kernel(pre_ref, rw_ref, ids_ref, cot_ref, out_ref, *, hid, cut):
    per, tokens = ids_ref.shape
    slots = per * tokens
    rows, _ = out_ref.shape
    ids_col = by_slot(ids_ref[...].astype(F32), tokens)
    ids_row = ids_col.T
    i, j = iota((slots, slots), 0), iota((slots, slots), 1)
    earlier = jnp.where((ids_col == ids_row) & (i < j), 1.0, 0.0)
    place = ids_row[0:1] * (2.0 * CAP) + jnp.sum(earlier, axis=0, keepdims=True)
    place = place.astype(jnp.int32)
    r = iota((rows, slots), 0)
    first = jnp.where(r == place, 1.0, 0.0).astype(BF16)
    second = jnp.where(r == place + CAP, 1.0, 0.0).astype(BF16)
    of_token = jnp.where(iota((slots, tokens), 0) // per == iota((slots, tokens), 1), 1.0, 0.0).astype(BF16)
    first_tok = mm(first, of_token).astype(BF16)
    second_tok = mm(second, of_token).astype(BF16)
    gate, up, sig = gate_terms(pre_ref, hid)
    weight = by_slot(rw_ref[...], tokens)[:, 0:1]
    hidden = (gate * sig * up * weight).astype(BF16)
    d = cot_ref.shape[1]
    out_ref[:, :hid] = (mm(first, hidden) + mm(second_tok, cot_ref[:, cut : cut + hid])).astype(BF16)
    out_ref[:, hid:] = (
        mm(first_tok, cot_ref[:, :cut]) + mm(second_tok, cot_ref[:, cut + hid : d])
    ).astype(BF16)


def expert_kernel(core_ref, x_ref, w_ref, y_ref, keep_ref, send_ref, cot, hid_rows, outs, grad, *, hid, cut, step):
    n = pl.program_id(0)
    rows, _ = x_ref.shape
    half = rows // 2
    d = cot.shape[1]

    @pl.when(n == 0)
    def _():
        m, r = iota((half, rows), 0), iota((half, rows), 1)
        spot = (m // CAP) * (2 * CAP) + m % CAP
        first = jnp.where(r == spot, 1.0, 0.0).astype(BF16)
        second = jnp.where(r == spot + CAP, 1.0, 0.0).astype(BF16)
        hid_rows[...] = mm(first, x_ref[:, :hid]).astype(BF16)
        cot[:, :cut] = mm(first, x_ref[:, hid:]).astype(BF16)
        cot[:, cut:] = mm(second, x_ref[...]).astype(BF16)
        grad[...] = jnp.zeros_like(grad)

    at = pl.multiple_of(n * step, step)
    piece = step // 2
    core = core_ref[0]
    hidden = hid_rows[...]
    weight = w_ref[...]
    grad[...] += mm(cot[:, pl.ds(at, step)], weight)
    outs[:, pl.ds(at, step)] = mm(hidden, weight, ((1,), (1,))).astype(BF16)
    mine = pl.multiple_of(at + core * piece, piece)
    other = pl.multiple_of(at + (1 - core) * piece, piece)
    send_ref[...] = mm(cot[:, pl.ds(other, piece)], hidden, ((0,), (0,))).astype(BF16)
    keep_ref[...] = mm(cot[:, pl.ds(mine, piece)], hidden, ((0,), (0,))).astype(BF16)

    @pl.when(n == pl.num_programs(0) - 1)
    def _():
        r, m = iota((rows, half), 0), iota((rows, half), 1)
        spot = (m // CAP) * (2 * CAP) + m % CAP
        first = jnp.where(r == spot, 1.0, 0.0).astype(BF16)
        second = jnp.where(r == spot + CAP, 1.0, 0.0).astype(BF16)
        y_ref[:, :hid] = (
            mm(first, grad[...].astype(BF16)) + mm(second, outs[:, cut : cut + hid])
        ).astype(BF16)
        y_ref[:, hid:] = (mm(first, outs[:, :cut]) + mm(second, outs[:, cut + hid : d])).astype(BF16)


def finish_kernel(y_ref, pre_ref, rw_ref, ids_ref, mixed_ref, route_ref, grads_ref, *, hid, cut):
    per, tokens = ids_ref.shape
    slots = per * tokens
    rows, _ = y_ref.shape
    ids_col = by_slot(ids_ref[...].astype(F32), tokens)
    ids_row = ids_col.T
    i, j = iota((slots, slots), 0), iota((slots, slots), 1)
    earlier = jnp.where((ids_col == ids_row) & (j < i), 1.0, 0.0)
    place = ids_col[:, 0:1] * (2.0 * CAP) + jnp.sum(earlier, axis=1, keepdims=True)
    place = place.astype(jnp.int32)
    r = iota((slots, rows), 1)
    first = jnp.where(r == place, 1.0, 0.0).astype(BF16)
    second = jnp.where(r == place + CAP, 1.0, 0.0).astype(BF16)
    of_token = jnp.where(iota((tokens, slots), 1) // per == iota((tokens, slots), 0), 1.0, 0.0).astype(BF16)
    first_tok = mm(of_token, first).astype(BF16)
    second_tok = mm(of_token, second).astype(BF16)
    grad = mm(first, y_ref[:, :hid])
    mixed_ref[:, :cut] = mm(first_tok, y_ref[:, hid:]).astype(BF16)
    mixed_ref[:, cut:] = mm(second_tok, y_ref[...]).astype(BF16)
    gate, up, sig = gate_terms(pre_ref, hid)
    act = gate * sig
    hidden = (act * up).astype(BF16).astype(F32)
    total = jnp.sum(grad * hidden, axis=1, keepdims=True)
    spread = jnp.broadcast_to(total, (slots, 128)).reshape(tokens, per, 128)
    lane, tok = iota((tokens, per, 128), 2), iota((tokens, per, 128), 0)
    route_ref[...] = jnp.sum(jnp.where(lane == tok, spread, 0.0), axis=0)[:, :tokens]
    scaled = grad * by_slot(rw_ref[...], tokens)[:, 0:1]
    grads_ref[:, :hid] = (scaled * up * (sig * (1.0 + gate * (1.0 - sig)))).astype(BF16)
    grads_ref[:, hid:] = (scaled * act).astype(BF16)


def on_device(preactivations, route_weights, expert_ids, down_proj, output_cotangent):
    tokens, per, pre_width = preactivations.shape
    hid = pre_width // 2
    d = output_cotangent.shape[1]
    experts = lax.axis_size(("y", "z"))
    group = lax.axis_size("x")
    rows = experts * 2 * CAP
    width = (hid + d) // 2
    cut = width - hid
    slots = tokens * per
    step = d // group
    piece = step // 2
    pre = preactivations.reshape(slots, pre_width)
    rw_t, ids_t = route_weights.T, expert_ids.T
    core = lax.axis_index("c").astype(jnp.int32).reshape(1)

    send = pl.pallas_call(
        functools.partial(prep_kernel, hid=hid, cut=cut),
        out_shape=jax.ShapeDtypeStruct((rows, width), BF16),
        name="prep",
    )(pre, rw_t, ids_t, output_cotangent)
    recv = lax.all_to_all(
        send.reshape(experts, 2 * CAP, width), ("y", "z"), split_axis=0, concat_axis=0, tiled=True
    ).reshape(rows, width)
    back, keep, give = pl.pallas_call(
        functools.partial(expert_kernel, hid=hid, cut=cut, step=step),
        out_shape=(
            jax.ShapeDtypeStruct((rows, width), BF16),
            jax.ShapeDtypeStruct((d // 2, hid), BF16),
            jax.ShapeDtypeStruct((d // 2, hid), BF16),
        ),
        grid_spec=pltpu.PrefetchScalarGridSpec(
            num_scalar_prefetch=1,
            grid=(group,),
            in_specs=[
                pl.BlockSpec((rows, width), lambda n, c: (0, 0)),
                pl.BlockSpec((step, hid), lambda n, c: (n, 0)),
            ],
            out_specs=(
                pl.BlockSpec((rows, width), lambda n, c: (0, 0)),
                pl.BlockSpec((piece, hid), lambda n, c: (n, 0)),
                pl.BlockSpec((piece, hid), lambda n, c: (n, 0)),
            ),
            scratch_shapes=[
                pltpu.VMEM((rows // 2, d), BF16),
                pltpu.VMEM((rows // 2, hid), BF16),
                pltpu.VMEM((rows // 2, d), BF16),
                pltpu.VMEM((rows // 2, hid), F32),
            ],
        ),
        name="expert",
    )(core, recv, down_proj[0])
    got = lax.ppermute(give, "c", [(0, 1), (1, 0)])
    home = lax.all_to_all(
        back.reshape(experts, 2 * CAP, width), ("y", "z"), split_axis=0, concat_axis=0, tiled=True
    ).reshape(rows, width)
    pair = (keep.astype(F32) + got.astype(F32)).astype(BF16)
    weight_grads = lax.psum_scatter(pair, "x", scatter_dimension=0, tiled=True).astype(F32)
    mixed, route_t, grads = pl.pallas_call(
        functools.partial(finish_kernel, hid=hid, cut=cut),
        out_shape=(
            jax.ShapeDtypeStruct((tokens, d), BF16),
            jax.ShapeDtypeStruct((per, tokens), F32),
            jax.ShapeDtypeStruct((slots, pre_width), BF16),
        ),
        name="finish",
    )(home, pre, rw_t, ids_t)
    return mixed, route_t.T, grads.reshape(tokens, per, pre_width), weight_grads[None]


def solution(mesh):
    fine = Mesh(mesh.devices.reshape(8, 2, 8, 8), ("x", "c", "y", "z"))
    every = ("x", "c", "y", "z")
    in_specs = (
        P(every, None, None),
        P(every, None),
        P(every, None),
        P(("y", "z"), None, None),
        P(every, None),
    )
    out_specs = (
        P(every, None),
        P(every, None),
        P(every, None, None),
        P(("y", "z"), ("x", "c"), None),
    )
    return jax.shard_map(
        on_device, mesh=fine, in_specs=in_specs, out_specs=out_specs, check_vma=False
    )
```

```python
import functools

import jax
import jax.numpy as jnp
from jax import lax
from jax.experimental import pallas as pl
from jax.experimental.pallas import tpu as pltpu
from jax.sharding import Mesh, PartitionSpec as P


F32 = jnp.float32
BF16 = jnp.bfloat16
CAP = 4


def iota(shape, dim):
    return lax.broadcasted_iota(jnp.int32, shape, dim)


def mm(a, b, dims=((1,), (0,))):
    return lax.dot_general(a, b, (dims, ((), ())), preferred_element_type=F32)


def by_slot(values_t, tokens):
    return jnp.concatenate(
        [jnp.broadcast_to(values_t[:, t : t + 1], (values_t.shape[0], 128)) for t in range(tokens)],
        axis=0,
    )


def gate_terms(pre_ref, hid):
    gate = pre_ref[:, :hid].astype(F32)
    up = pre_ref[:, hid:].astype(F32)
    sig = jax.nn.sigmoid(gate)
    return gate, up, sig


def prep_kernel(core_ref, pre_ref, rw_ref, ids_ref, cot_ref, out_ref, *, hid, cut):
    per, tokens = ids_ref.shape
    slots = per * tokens
    rows, _ = out_ref.shape
    ids_col = by_slot(ids_ref[...].astype(F32), tokens)
    ids_row = ids_col.T
    i, j = iota((slots, slots), 0), iota((slots, slots), 1)
    earlier = jnp.where((ids_col == ids_row) & (i < j), 1.0, 0.0)
    place = ids_row[0:1] * (2.0 * CAP) + jnp.sum(earlier, axis=0, keepdims=True)
    place = place.astype(jnp.int32)
    r = iota((rows, slots), 0)
    first = jnp.where(r == place, 1.0, 0.0).astype(BF16)
    second = jnp.where(r == place + CAP, 1.0, 0.0).astype(BF16)
    of_token = jnp.where(iota((slots, tokens), 0) // per == iota((slots, tokens), 1), 1.0, 0.0).astype(BF16)
    first_tok = mm(first, of_token).astype(BF16)
    second_tok = mm(second, of_token).astype(BF16)
    gate, up, sig = gate_terms(pre_ref, hid)
    weight = by_slot(rw_ref[...], tokens)[:, 0:1]
    hidden = (gate * sig * up * weight).astype(BF16)
    d = cot_ref.shape[1]
    out_ref[:, :hid] = (mm(first, hidden) + mm(second_tok, cot_ref[:, cut : cut + hid])).astype(BF16)
    out_ref[:, hid:] = (
        mm(first_tok, cot_ref[:, :cut]) + mm(second_tok, cot_ref[:, cut + hid : d])
    ).astype(BF16)


def expert_kernel(core_ref, x_ref, w_ref, y_ref, mine_ref, give_ref, cot, outs, grad, *, hid, cut, step):
    n = pl.program_id(0)
    rows, _ = x_ref.shape
    half = rows // 2
    d = cot.shape[1]

    @pl.when(n == 0)
    def _():
        m, r = iota((half, rows), 0), iota((half, rows), 1)
        spot = (m // CAP) * (2 * CAP) + m % CAP
        first = jnp.where(r == spot, 1.0, 0.0).astype(BF16)
        second = jnp.where(r == spot + CAP, 1.0, 0.0).astype(BF16)
        hidden = mm(first, x_ref[:, :hid]).astype(BF16)
        mine_ref[:, :hid] = hidden
        give_ref[:, :hid] = hidden
        cot[:, :cut] = mm(first, x_ref[:, hid:]).astype(BF16)
        cot[:, cut:] = mm(second, x_ref[...]).astype(BF16)
        grad[...] = jnp.zeros_like(grad)

    at = pl.multiple_of(n * step, step)
    piece = step // 2
    core = core_ref[0]
    weight = w_ref[...]
    grad[...] += mm(cot[:, pl.ds(at, step)], weight)
    outs[:, pl.ds(at, step)] = mm(mine_ref[:, :hid], weight, ((1,), (1,))).astype(BF16)
    to = pl.multiple_of(hid + n * piece, piece)
    mine_ref[:, pl.ds(to, piece)] = cot[:, pl.ds(pl.multiple_of(at + core * piece, piece), piece)]
    give_ref[:, pl.ds(to, piece)] = cot[:, pl.ds(pl.multiple_of(at + (1 - core) * piece, piece), piece)]

    @pl.when(n == pl.num_programs(0) - 1)
    def _():
        r, m = iota((rows, half), 0), iota((rows, half), 1)
        spot = (m // CAP) * (2 * CAP) + m % CAP
        first = jnp.where(r == spot, 1.0, 0.0).astype(BF16)
        second = jnp.where(r == spot + CAP, 1.0, 0.0).astype(BF16)
        y_ref[:, :hid] = (
            mm(first, grad[...].astype(BF16)) + mm(second, outs[:, cut : cut + hid])
        ).astype(BF16)
        y_ref[:, hid:] = (mm(first, outs[:, :cut]) + mm(second, outs[:, cut + hid : d])).astype(BF16)


def weight_kernel(mine_ref, got_ref, out_ref, *, hid, piece):
    n = pl.program_id(0)
    to = pl.multiple_of(hid + n * piece, piece)
    out_ref[...] = (
        mm(mine_ref[:, pl.ds(to, piece)], mine_ref[:, :hid], ((0,), (0,)))
        + mm(got_ref[:, pl.ds(to, piece)], got_ref[:, :hid], ((0,), (0,)))
    ).astype(BF16)


def finish_kernel(y_ref, pre_ref, rw_ref, ids_ref, sum_ref, mixed_ref, route_ref, grads_ref, down_ref, *, hid, cut):
    down_ref[...] = sum_ref[...].astype(F32)
    per, tokens = ids_ref.shape
    slots = per * tokens
    rows, _ = y_ref.shape
    ids_col = by_slot(ids_ref[...].astype(F32), tokens)
    ids_row = ids_col.T
    i, j = iota((slots, slots), 0), iota((slots, slots), 1)
    earlier = jnp.where((ids_col == ids_row) & (j < i), 1.0, 0.0)
    place = ids_col[:, 0:1] * (2.0 * CAP) + jnp.sum(earlier, axis=1, keepdims=True)
    place = place.astype(jnp.int32)
    r = iota((slots, rows), 1)
    first = jnp.where(r == place, 1.0, 0.0).astype(BF16)
    second = jnp.where(r == place + CAP, 1.0, 0.0).astype(BF16)
    of_token = jnp.where(iota((tokens, slots), 1) // per == iota((tokens, slots), 0), 1.0, 0.0).astype(BF16)
    first_tok = mm(of_token, first).astype(BF16)
    second_tok = mm(of_token, second).astype(BF16)
    grad = mm(first, y_ref[:, :hid])
    mixed_ref[:, :cut] = mm(first_tok, y_ref[:, hid:]).astype(BF16)
    mixed_ref[:, cut:] = mm(second_tok, y_ref[...]).astype(BF16)
    gate, up, sig = gate_terms(pre_ref, hid)
    act = gate * sig
    hidden = (act * up).astype(BF16).astype(F32)
    total = jnp.sum(grad * hidden, axis=1, keepdims=True)
    spread = jnp.broadcast_to(total, (slots, 128)).reshape(tokens, per, 128)
    lane, tok = iota((tokens, per, 128), 2), iota((tokens, per, 128), 0)
    route_ref[...] = jnp.sum(jnp.where(lane == tok, spread, 0.0), axis=0)[:, :tokens]
    scaled = grad * by_slot(rw_ref[...], tokens)[:, 0:1]
    grads_ref[:, :hid] = (scaled * up * (sig * (1.0 + gate * (1.0 - sig)))).astype(BF16)
    grads_ref[:, hid:] = (scaled * act).astype(BF16)


def on_device(preactivations, route_weights, expert_ids, down_proj, output_cotangent):
    tokens, per, pre_width = preactivations.shape
    hid = pre_width // 2
    d = output_cotangent.shape[1]
    experts = lax.axis_size(("y", "z"))
    group = lax.axis_size("x")
    rows = experts * 2 * CAP
    width = (hid + d) // 2
    cut = width - hid
    slots = tokens * per
    step = d // group
    piece = step // 2
    pre = preactivations.reshape(slots, pre_width)
    rw_t, ids_t = route_weights.T, expert_ids.T
    core = lax.axis_index("c").astype(jnp.int32).reshape(1)

    whole = pl.BlockSpec((rows // 2, hid + d // 2), lambda n, *_: (0, 0))

    send = pl.pallas_call(
        functools.partial(prep_kernel, hid=hid, cut=cut),
        out_shape=jax.ShapeDtypeStruct((rows, width), BF16),
        in_specs=[pl.BlockSpec(memory_space=pltpu.SMEM)] + [pl.BlockSpec(memory_space=pltpu.VMEM)] * 4,
        name="prep",
    )(core, pre, rw_t, ids_t, output_cotangent)
    recv = lax.all_to_all(
        send.reshape(experts, 2 * CAP, width), ("y", "z"), split_axis=0, concat_axis=0, tiled=True
    ).reshape(rows, width)
    recv = pltpu.with_memory_space_constraint(recv, pltpu.VMEM)
    back, mine, give = pl.pallas_call(
        functools.partial(expert_kernel, hid=hid, cut=cut, step=step),
        out_shape=(
            jax.ShapeDtypeStruct((rows, width), BF16),
            jax.ShapeDtypeStruct((rows // 2, hid + d // 2), BF16),
            jax.ShapeDtypeStruct((rows // 2, hid + d // 2), BF16),
        ),
        grid_spec=pltpu.PrefetchScalarGridSpec(
            num_scalar_prefetch=1,
            grid=(group,),
            in_specs=[
                pl.BlockSpec(memory_space=pltpu.VMEM),
                pl.BlockSpec((step, hid), lambda n, c: (n, 0)),
            ],
            out_specs=(pl.BlockSpec((rows, width), lambda n, c: (0, 0)), whole, whole),
            scratch_shapes=[
                pltpu.VMEM((rows // 2, d), BF16),
                pltpu.VMEM((rows // 2, d), BF16),
                pltpu.VMEM((rows // 2, hid), F32),
            ],
        ),
        name="expert",
    )(core, recv, down_proj[0])
    got = lax.ppermute(give, "c", [(0, 1), (1, 0)])
    home = lax.all_to_all(
        back.reshape(experts, 2 * CAP, width), ("y", "z"), split_axis=0, concat_axis=0, tiled=True
    ).reshape(rows, width)
    home = pltpu.with_memory_space_constraint(home, pltpu.VMEM)
    pair = pl.pallas_call(
        functools.partial(weight_kernel, hid=hid, piece=piece),
        out_shape=jax.ShapeDtypeStruct((d // 2, hid), BF16),
        grid=(group,),
        in_specs=[whole, whole],
        out_specs=pl.BlockSpec((piece, hid), lambda n: (n, 0)),
        name="weights",
    )(mine, got)
    weight_sum = lax.psum_scatter(pair, "x", scatter_dimension=0, tiled=True)
    mixed, route_t, grads, down = pl.pallas_call(
        functools.partial(finish_kernel, hid=hid, cut=cut),
        out_shape=(
            jax.ShapeDtypeStruct((tokens, d), BF16),
            jax.ShapeDtypeStruct((per, tokens), F32),
            jax.ShapeDtypeStruct((slots, pre_width), BF16),
            jax.ShapeDtypeStruct((piece, hid), F32),
        ),
        name="finish",
    )(home, pre, rw_t, ids_t, weight_sum)
    return mixed, route_t.T, grads.reshape(tokens, per, pre_width), down[None]


def solution(mesh):
    fine = Mesh(mesh.devices.reshape(8, 2, 8, 8), ("x", "c", "y", "z"))
    every = ("x", "c", "y", "z")
    in_specs = (
        P(every, None, None),
        P(every, None),
        P(every, None),
        P(("y", "z"), None, None),
        P(every, None),
    )
    out_specs = (
        P(every, None),
        P(every, None),
        P(every, None, None),
        P(("y", "z"), ("x", "c"), None),
    )
    return jax.shard_map(
        on_device, mesh=fine, in_specs=in_specs, out_specs=out_specs, check_vma=False
    )
```

```python
import functools

import jax
import jax.numpy as jnp
from jax import lax
from jax.experimental import pallas as pl
from jax.experimental.pallas import tpu as pltpu
from jax.sharding import Mesh, PartitionSpec as P


F32 = jnp.float32
BF16 = jnp.bfloat16
CAP = 4


def iota(shape, dim):
    return lax.broadcasted_iota(jnp.int32, shape, dim)


def mm(a, b, dims=((1,), (0,))):
    return lax.dot_general(a, b, (dims, ((), ())), preferred_element_type=F32)


def by_slot(values_t, tokens):
    return jnp.concatenate(
        [jnp.broadcast_to(values_t[:, t : t + 1], (values_t.shape[0], 128)) for t in range(tokens)],
        axis=0,
    )


def halves(block):
    rows, w = block.shape
    pairs = block.astype(F32).reshape(rows // 16, 2, 8, w)
    a, b = pairs[:, 0], pairs[:, 1]
    low = iota((rows // 16, 8, w), 1) < CAP
    first = jnp.where(low, a, pltpu.roll(b, CAP, 1))
    second = jnp.where(low, pltpu.roll(a, CAP, 1), b)
    return first.reshape(rows // 2, w), second.reshape(rows // 2, w)


def weave(first, second):
    half, w = first.shape
    a, b = first.reshape(half // 8, 8, w), second.reshape(half // 8, 8, w)
    low = iota((half // 8, 8, w), 1) < CAP
    top = jnp.where(low, a, pltpu.roll(b, CAP, 1))
    bottom = jnp.where(low, pltpu.roll(a, CAP, 1), b)
    return jnp.stack([top, bottom], axis=1).reshape(half * 2, w).astype(BF16)


def gate_terms(pre_ref, hid):
    gate = pre_ref[:, :hid].astype(F32)
    up = pre_ref[:, hid:].astype(F32)
    sig = jax.nn.sigmoid(gate)
    return gate, up, sig


def prep_kernel(core_ref, pre_ref, rw_ref, ids_ref, cot_ref, out_ref, *, hid, cut):
    per, tokens = ids_ref.shape
    slots = per * tokens
    rows, _ = out_ref.shape
    ids_col = by_slot(ids_ref[...].astype(F32), tokens)
    ids_row = ids_col.T
    i, j = iota((slots, slots), 0), iota((slots, slots), 1)
    earlier = jnp.where((ids_col == ids_row) & (i < j), 1.0, 0.0)
    place = ids_row[0:1] * (2.0 * CAP) + jnp.sum(earlier, axis=0, keepdims=True)
    place = place.astype(jnp.int32)
    r = iota((rows, slots), 0)
    first = jnp.where(r == place, 1.0, 0.0).astype(BF16)
    second = jnp.where(r == place + CAP, 1.0, 0.0).astype(BF16)
    of_token = jnp.where(iota((slots, tokens), 0) // per == iota((slots, tokens), 1), 1.0, 0.0).astype(BF16)
    first_tok = mm(first, of_token).astype(BF16)
    second_tok = mm(second, of_token).astype(BF16)
    gate, up, sig = gate_terms(pre_ref, hid)
    weight = by_slot(rw_ref[...], tokens)[:, 0:1]
    hidden = (gate * sig * up * weight).astype(BF16)
    d = cot_ref.shape[1]
    out_ref[:, :hid] = mm(
        jnp.concatenate([first, second_tok], axis=1),
        jnp.concatenate([hidden, cot_ref[:, cut : cut + hid]], axis=0),
    ).astype(BF16)
    out_ref[:, hid:] = mm(
        jnp.concatenate([first_tok, second_tok], axis=1),
        jnp.concatenate([cot_ref[:, :cut], cot_ref[:, cut + hid : d]], axis=0),
    ).astype(BF16)


def expert_kernel(core_ref, x_ref, w_ref, y_ref, mine_ref, give_ref, cot, outs, grad, *, hid, cut, step):
    n = pl.program_id(0)
    _, width = x_ref.shape

    @pl.when(n == 0)
    def _():
        for at in range(0, width, 128):
            first, second = halves(x_ref[:, at : at + 128])
            first = first.astype(BF16)
            if at < hid:
                mine_ref[:, at : at + 128] = first
                give_ref[:, at : at + 128] = first
            else:
                cot[:, at - hid : at - hid + 128] = first
            cot[:, cut + at : cut + at + 128] = second.astype(BF16)
        grad[...] = jnp.zeros_like(grad)

    at = pl.multiple_of(n * step, step)
    piece = step // 2
    core = core_ref[0]
    weight = w_ref[...]
    grad[...] += mm(cot[:, pl.ds(at, step)], weight)
    outs[:, pl.ds(at, step)] = mm(mine_ref[:, :hid], weight, ((1,), (1,)))
    to = pl.multiple_of(hid + n * piece, piece)
    mine_ref[:, pl.ds(to, piece)] = cot[:, pl.ds(pl.multiple_of(at + core * piece, piece), piece)]
    give_ref[:, pl.ds(to, piece)] = cot[:, pl.ds(pl.multiple_of(at + (1 - core) * piece, piece), piece)]

    @pl.when(n == pl.num_programs(0) - 1)
    def _():
        for at in range(0, width, 128):
            first = grad[:, at : at + 128] if at < hid else outs[:, at - hid : at - hid + 128]
            y_ref[:, at : at + 128] = weave(first, outs[:, cut + at : cut + at + 128])


def weight_kernel(mine_ref, got_ref, out_ref, *, hid, piece):
    n = pl.program_id(0)
    to = pl.multiple_of(hid + n * piece, piece)
    out_ref[...] = (
        mm(mine_ref[:, pl.ds(to, piece)], mine_ref[:, :hid], ((0,), (0,)))
        + mm(got_ref[:, pl.ds(to, piece)], got_ref[:, :hid], ((0,), (0,)))
    ).astype(BF16)


def finish_kernel(y_ref, pre_ref, rw_ref, ids_ref, sum_ref, mixed_ref, route_ref, grads_ref, down_ref, *, hid, cut):
    down_ref[...] = sum_ref[...].astype(F32)
    per, tokens = ids_ref.shape
    slots = per * tokens
    rows, _ = y_ref.shape
    ids_col = by_slot(ids_ref[...].astype(F32), tokens)
    ids_row = ids_col.T
    i, j = iota((slots, slots), 0), iota((slots, slots), 1)
    earlier = jnp.where((ids_col == ids_row) & (j < i), 1.0, 0.0)
    place = ids_col[:, 0:1] * (2.0 * CAP) + jnp.sum(earlier, axis=1, keepdims=True)
    place = place.astype(jnp.int32)
    r = iota((slots, rows), 1)
    first = jnp.where(r == place, 1.0, 0.0).astype(BF16)
    second = jnp.where(r == place + CAP, 1.0, 0.0).astype(BF16)
    of_token = jnp.where(iota((tokens, slots), 1) // per == iota((tokens, slots), 0), 1.0, 0.0).astype(BF16)
    first_tok = mm(of_token, first).astype(BF16)
    second_tok = mm(of_token, second).astype(BF16)
    both = jnp.concatenate([first_tok, second_tok], axis=0)
    left = mm(jnp.concatenate([first, both], axis=0), y_ref[:, :hid])
    right = mm(both, y_ref[:, hid:])
    grad = left[:slots]
    mixed_ref[:, :cut] = right[:tokens].astype(BF16)
    mixed_ref[:, cut : cut + hid] = left[slots + tokens :].astype(BF16)
    mixed_ref[:, cut + hid :] = right[tokens:].astype(BF16)
    gate, up, sig = gate_terms(pre_ref, hid)
    act = gate * sig
    hidden = (act * up).astype(BF16).astype(F32)
    total = jnp.sum(grad * hidden, axis=1, keepdims=True)
    spread = jnp.broadcast_to(total, (slots, 128)).reshape(tokens, per, 128)
    lane, tok = iota((tokens, per, 128), 2), iota((tokens, per, 128), 0)
    route_ref[...] = jnp.sum(jnp.where(lane == tok, spread, 0.0), axis=0)[:, :tokens]
    scaled = grad * by_slot(rw_ref[...], tokens)[:, 0:1]
    grads_ref[:, :hid] = (scaled * up * (sig * (1.0 + gate * (1.0 - sig)))).astype(BF16)
    grads_ref[:, hid:] = (scaled * act).astype(BF16)


def on_device(preactivations, route_weights, expert_ids, down_proj, output_cotangent):
    tokens, per, pre_width = preactivations.shape
    hid = pre_width // 2
    d = output_cotangent.shape[1]
    experts = lax.axis_size(("y", "z"))
    group = lax.axis_size("x")
    rows = experts * 2 * CAP
    width = (hid + d) // 2
    cut = width - hid
    slots = tokens * per
    step = d // group
    piece = step // 2
    pre = preactivations.reshape(slots, pre_width)
    rw_t, ids_t = route_weights.T, expert_ids.T
    core = lax.axis_index("c").astype(jnp.int32).reshape(1)

    whole = pl.BlockSpec((rows // 2, hid + d // 2), lambda n, *_: (0, 0))

    send = pl.pallas_call(
        functools.partial(prep_kernel, hid=hid, cut=cut),
        out_shape=jax.ShapeDtypeStruct((rows, width), BF16),
        in_specs=[pl.BlockSpec(memory_space=pltpu.SMEM)] + [pl.BlockSpec(memory_space=pltpu.VMEM)] * 4,
        name="prep",
    )(core, pre, rw_t, ids_t, output_cotangent)
    recv = lax.all_to_all(
        send.reshape(experts, 2 * CAP, width), ("y", "z"), split_axis=0, concat_axis=0, tiled=True
    ).reshape(rows, width)
    recv = pltpu.with_memory_space_constraint(recv, pltpu.VMEM)
    back, mine, give = pl.pallas_call(
        functools.partial(expert_kernel, hid=hid, cut=cut, step=step),
        out_shape=(
            jax.ShapeDtypeStruct((rows, width), BF16),
            jax.ShapeDtypeStruct((rows // 2, hid + d // 2), BF16),
            jax.ShapeDtypeStruct((rows // 2, hid + d // 2), BF16),
        ),
        grid_spec=pltpu.PrefetchScalarGridSpec(
            num_scalar_prefetch=1,
            grid=(group,),
            in_specs=[
                pl.BlockSpec(memory_space=pltpu.VMEM),
                pl.BlockSpec((step, hid), lambda n, c: (n, 0)),
            ],
            out_specs=(pl.BlockSpec((rows, width), lambda n, c: (0, 0)), whole, whole),
            scratch_shapes=[
                pltpu.VMEM((rows // 2, d), BF16),
                pltpu.VMEM((rows // 2, d), F32),
                pltpu.VMEM((rows // 2, hid), F32),
            ],
        ),
        name="expert",
    )(core, recv, down_proj[0])
    got = lax.ppermute(give, "c", [(0, 1), (1, 0)])
    home = lax.all_to_all(
        back.reshape(experts, 2 * CAP, width), ("y", "z"), split_axis=0, concat_axis=0, tiled=True
    ).reshape(rows, width)
    home = pltpu.with_memory_space_constraint(home, pltpu.VMEM)
    pair = pl.pallas_call(
        functools.partial(weight_kernel, hid=hid, piece=piece),
        out_shape=jax.ShapeDtypeStruct((d // 2, hid), BF16),
        grid=(group,),
        in_specs=[whole, whole],
        out_specs=pl.BlockSpec((piece, hid), lambda n: (n, 0)),
        name="weights",
    )(mine, got)
    weight_sum = lax.psum_scatter(pair, "x", scatter_dimension=0, tiled=True)
    mixed, route_t, grads, down = pl.pallas_call(
        functools.partial(finish_kernel, hid=hid, cut=cut),
        out_shape=(
            jax.ShapeDtypeStruct((tokens, d), BF16),
            jax.ShapeDtypeStruct((per, tokens), F32),
            jax.ShapeDtypeStruct((slots, pre_width), BF16),
            jax.ShapeDtypeStruct((piece, hid), F32),
        ),
        name="finish",
    )(home, pre, rw_t, ids_t, weight_sum)
    return mixed, route_t.T, grads.reshape(tokens, per, pre_width), down[None]


def solution(mesh):
    fine = Mesh(mesh.devices.reshape(8, 2, 8, 8), ("x", "c", "y", "z"))
    every = ("x", "c", "y", "z")
    in_specs = (
        P(every, None, None),
        P(every, None),
        P(every, None),
        P(("y", "z"), None, None),
        P(every, None),
    )
    out_specs = (
        P(every, None),
        P(every, None),
        P(every, None, None),
        P(("y", "z"), ("x", "c"), None),
    )
    return jax.shard_map(
        on_device, mesh=fine, in_specs=in_specs, out_specs=out_specs, check_vma=False
    )
```

```python
import functools

import jax
import jax.numpy as jnp
from jax import lax
from jax.experimental import pallas as pl
from jax.experimental.pallas import tpu as pltpu
from jax.sharding import Mesh, PartitionSpec as P


F32 = jnp.float32
BF16 = jnp.bfloat16
CAP = 4


def iota(shape, dim):
    return lax.broadcasted_iota(jnp.int32, shape, dim)


def mm(a, b, dims=((1,), (0,))):
    return lax.dot_general(a, b, (dims, ((), ())), preferred_element_type=F32)


def by_slot(values_t, tokens):
    return jnp.concatenate(
        [jnp.broadcast_to(values_t[:, t : t + 1], (values_t.shape[0], 128)) for t in range(tokens)],
        axis=0,
    )


def halves(block):
    rows, w = block.shape
    pairs = block.astype(F32).reshape(rows // 16, 2, 8, w)
    a, b = pairs[:, 0], pairs[:, 1]
    low = iota((rows // 16, 8, w), 1) < CAP
    first = jnp.where(low, a, pltpu.roll(b, CAP, 1))
    second = jnp.where(low, pltpu.roll(a, CAP, 1), b)
    return first.reshape(rows // 2, w), second.reshape(rows // 2, w)


def weave(first, second):
    half, w = first.shape
    a, b = first.reshape(half // 8, 8, w), second.reshape(half // 8, 8, w)
    low = iota((half // 8, 8, w), 1) < CAP
    top = jnp.where(low, a, pltpu.roll(b, CAP, 1))
    bottom = jnp.where(low, pltpu.roll(a, CAP, 1), b)
    return jnp.stack([top, bottom], axis=1).reshape(half * 2, w).astype(BF16)


CHUNKS = (0, 1280, 1920, 2432)


def chunk_copy(made, out_ref, sems, n, at, to):
    return pltpu.make_async_copy(made.at[:, at:to], out_ref.at[:, at:to], sems.at[n])


def gate_terms(pre_ref, hid):
    gate = pre_ref[:, :hid].astype(F32)
    up = pre_ref[:, hid:].astype(F32)
    sig = jax.nn.sigmoid(gate)
    return gate, up, sig


def prep_kernel(core_ref, pre_ref, rw_ref, ids_ref, cot_ref, out_ref, made, sems, *, hid, cut):
    per, tokens = ids_ref.shape
    slots = per * tokens
    rows, _ = out_ref.shape
    ids_col = by_slot(ids_ref[...].astype(F32), tokens)
    ids_row = ids_col.T
    i, j = iota((slots, slots), 0), iota((slots, slots), 1)
    earlier = jnp.where((ids_col == ids_row) & (i < j), 1.0, 0.0)
    place = ids_row[0:1] * (2.0 * CAP) + jnp.sum(earlier, axis=0, keepdims=True)
    place = place.astype(jnp.int32)
    r = iota((rows, slots), 0)
    first = jnp.where(r == place, 1.0, 0.0).astype(BF16)
    second = jnp.where(r == place + CAP, 1.0, 0.0).astype(BF16)
    of_token = jnp.where(iota((slots, tokens), 0) // per == iota((slots, tokens), 1), 1.0, 0.0).astype(BF16)
    first_tok = mm(first, of_token).astype(BF16)
    second_tok = mm(second, of_token).astype(BF16)
    left = jnp.concatenate([first_tok, second_tok], axis=1)
    copies = []
    for at, to in zip((hid,) + CHUNKS[1:-1], CHUNKS[1:]):
        made[:, at:to] = mm(
            left, jnp.concatenate([cot_ref[:, at - hid : to - hid], cot_ref[:, cut + at : cut + to]], axis=0)
        ).astype(BF16)
        copies.append(chunk_copy(made, out_ref, sems, len(copies), at, to))
        copies[-1].start()
    gate, up, sig = gate_terms(pre_ref, hid)
    weight = by_slot(rw_ref[...], tokens)[:, 0:1]
    hidden = (gate * sig * up * weight).astype(BF16)
    made[:, :hid] = mm(
        jnp.concatenate([first, second_tok], axis=1),
        jnp.concatenate([hidden, cot_ref[:, cut : cut + hid]], axis=0),
    ).astype(BF16)
    copies.append(chunk_copy(made, out_ref, sems, len(copies), 0, hid))
    copies[-1].start()
    for copy in copies:
        copy.wait()


def expert_kernel(
    core_ref, x_ref, w_ref, y_ref, mine_ref, give_ref, cot, outs, grad, made, kept, gift, w_buf, w_sems, y_sems, mine_sem, give_sem,
    *, hid, cut, step,
):
    _, width = x_ref.shape
    steps = cot.shape[1] // step
    piece = step // 2
    core = core_ref[0]

    def fetch(n):
        at = pl.multiple_of(n * step, step)
        return pltpu.make_async_copy(w_ref.at[pl.ds(at, step)], w_buf.at[pl.ds(at, step)], w_sems.at[n])

    for n in range(steps):
        fetch(n).start()
    for at in range(0, width, 128):
        first, second = halves(x_ref[:, at : at + 128])
        first = first.astype(BF16)
        if at < hid:
            kept[:, at : at + 128] = first
            gift[:, at : at + 128] = first
        else:
            cot[:, at - hid : at - hid + 128] = first
        cot[:, cut + at : cut + at + 128] = second.astype(BF16)
    grad[...] = jnp.zeros_like(grad)

    @pl.loop(0, steps)
    def _(n):
        fetch(n).wait()
        at = pl.multiple_of(n * step, step)
        weight = w_buf[pl.ds(at, step), :]
        grad[...] += mm(cot[:, pl.ds(at, step)], weight)
        outs[:, pl.ds(at, step)] = mm(kept[:, :hid], weight, ((1,), (1,)))
        to = pl.multiple_of(hid + n * piece, piece)
        kept[:, pl.ds(to, piece)] = cot[:, pl.ds(pl.multiple_of(at + core * piece, piece), piece)]
        gift[:, pl.ds(to, piece)] = cot[:, pl.ds(pl.multiple_of(at + (1 - core) * piece, piece), piece)]

    copies = [
        pltpu.make_async_copy(gift, give_ref, give_sem),
        pltpu.make_async_copy(kept, mine_ref, mine_sem),
    ]
    copies[0].start()
    copies[1].start()
    for k in range(len(CHUNKS) - 1):
        for at in range(CHUNKS[k], CHUNKS[k + 1], 128):
            first = grad[:, at : at + 128] if at < hid else outs[:, at - hid : at - hid + 128]
            made[:, at : at + 128] = weave(first, outs[:, cut + at : cut + at + 128])
        copies.append(chunk_copy(made, y_ref, y_sems, k, CHUNKS[k], CHUNKS[k + 1]))
        copies[-1].start()
    for copy in copies:
        copy.wait()


def weight_kernel(mine_ref, got_ref, out_ref, *, hid, piece):
    n = pl.program_id(0)
    to = pl.multiple_of(hid + n * piece, 256)
    out_ref[...] = (
        mm(mine_ref[:, pl.ds(to, piece)], mine_ref[:, :hid], ((0,), (0,)))
        + mm(got_ref[:, pl.ds(to, piece)], got_ref[:, :hid], ((0,), (0,)))
    ).astype(BF16)


def finish_kernel(y_ref, pre_ref, rw_ref, ids_ref, sum_ref, mixed_ref, route_ref, grads_ref, down_ref, *, hid, cut):
    down_ref[...] = sum_ref[...].astype(F32)
    per, tokens = ids_ref.shape
    slots = per * tokens
    rows, _ = y_ref.shape
    ids_col = by_slot(ids_ref[...].astype(F32), tokens)
    ids_row = ids_col.T
    i, j = iota((slots, slots), 0), iota((slots, slots), 1)
    earlier = jnp.where((ids_col == ids_row) & (j < i), 1.0, 0.0)
    place = ids_col[:, 0:1] * (2.0 * CAP) + jnp.sum(earlier, axis=1, keepdims=True)
    place = place.astype(jnp.int32)
    r = iota((slots, rows), 1)
    first = jnp.where(r == place, 1.0, 0.0).astype(BF16)
    second = jnp.where(r == place + CAP, 1.0, 0.0).astype(BF16)
    of_token = jnp.where(iota((tokens, slots), 1) // per == iota((tokens, slots), 0), 1.0, 0.0).astype(BF16)
    first_tok = mm(of_token, first).astype(BF16)
    second_tok = mm(of_token, second).astype(BF16)
    both = jnp.concatenate([first_tok, second_tok], axis=0)
    left = mm(jnp.concatenate([first, both], axis=0), y_ref[:, :hid])
    right = mm(both, y_ref[:, hid:])
    grad = left[:slots]
    mixed_ref[:, :cut] = right[:tokens].astype(BF16)
    mixed_ref[:, cut : cut + hid] = left[slots + tokens :].astype(BF16)
    mixed_ref[:, cut + hid :] = right[tokens:].astype(BF16)
    gate, up, sig = gate_terms(pre_ref, hid)
    act = gate * sig
    hidden = (act * up).astype(BF16).astype(F32)
    total = jnp.sum(grad * hidden, axis=1, keepdims=True)
    spread = jnp.broadcast_to(total, (slots, 128)).reshape(tokens, per, 128)
    lane, tok = iota((tokens, per, 128), 2), iota((tokens, per, 128), 0)
    route_ref[...] = jnp.sum(jnp.where(lane == tok, spread, 0.0), axis=0)[:, :tokens]
    scaled = grad * by_slot(rw_ref[...], tokens)[:, 0:1]
    grads_ref[:, :hid] = (scaled * up * (sig * (1.0 + gate * (1.0 - sig)))).astype(BF16)
    grads_ref[:, hid:] = (scaled * act).astype(BF16)


def on_device(preactivations, route_weights, expert_ids, down_proj, output_cotangent):
    tokens, per, pre_width = preactivations.shape
    hid = pre_width // 2
    d = output_cotangent.shape[1]
    experts = lax.axis_size(("y", "z"))
    group = lax.axis_size("x")
    rows = experts * 2 * CAP
    width = (hid + d) // 2
    cut = width - hid
    slots = tokens * per
    step = d // group
    piece = step // 2
    pre = preactivations.reshape(slots, pre_width)
    rw_t, ids_t = route_weights.T, expert_ids.T
    core = lax.axis_index("c").astype(jnp.int32).reshape(1)

    smem, vmem = pl.BlockSpec(memory_space=pltpu.SMEM), pl.BlockSpec(memory_space=pltpu.VMEM)
    outside = pl.BlockSpec(memory_space=pl.ANY)

    send = pl.pallas_call(
        functools.partial(prep_kernel, hid=hid, cut=cut),
        out_shape=jax.ShapeDtypeStruct((rows, width), BF16),
        in_specs=[smem] + [vmem] * 4,
        out_specs=pl.BlockSpec(memory_space=pl.ANY),
        scratch_shapes=[pltpu.VMEM((rows, width), BF16), pltpu.SemaphoreType.DMA((len(CHUNKS),))],
        name="prep",
    )(core, pre, rw_t, ids_t, output_cotangent)
    recv = lax.all_to_all(
        send.reshape(experts, 2 * CAP, width), ("y", "z"), split_axis=0, concat_axis=0, tiled=True
    ).reshape(rows, width)
    recv = pltpu.with_memory_space_constraint(recv, pltpu.VMEM)
    back, mine, give = pl.pallas_call(
        functools.partial(expert_kernel, hid=hid, cut=cut, step=step),
        out_shape=(
            jax.ShapeDtypeStruct((rows, width), BF16),
            jax.ShapeDtypeStruct((rows // 2, hid + d // 2), BF16),
            jax.ShapeDtypeStruct((rows // 2, hid + d // 2), BF16),
        ),
        in_specs=[smem, vmem, outside],
        out_specs=(outside, outside, outside),
        scratch_shapes=[
            pltpu.VMEM((rows // 2, d), BF16),
            pltpu.VMEM((rows // 2, d), F32),
            pltpu.VMEM((rows // 2, hid), F32),
            pltpu.VMEM((rows, width), BF16),
            pltpu.VMEM((rows // 2, hid + d // 2), BF16),
            pltpu.VMEM((rows // 2, hid + d // 2), BF16),
            pltpu.VMEM((d, hid), BF16),
            pltpu.SemaphoreType.DMA((group,)),
            pltpu.SemaphoreType.DMA((len(CHUNKS) - 1,)),
            pltpu.SemaphoreType.DMA,
            pltpu.SemaphoreType.DMA,
        ],
        name="expert",
    )(core, recv, down_proj[0])
    got = lax.ppermute(give, "c", [(0, 1), (1, 0)])
    home = lax.all_to_all(
        back.reshape(experts, 2 * CAP, width), ("y", "z"), split_axis=0, concat_axis=0, tiled=True
    ).reshape(rows, width)
    home = pltpu.with_memory_space_constraint(home, pltpu.VMEM)
    pair = pl.pallas_call(
        functools.partial(weight_kernel, hid=hid, piece=step),
        out_shape=jax.ShapeDtypeStruct((d // 2, hid), BF16),
        grid=(group // 2,),
        in_specs=[pl.BlockSpec((rows // 2, hid + d // 2), lambda n: (0, 0))] * 2,
        out_specs=pl.BlockSpec((step, hid), lambda n: (n, 0)),
        name="weights",
    )(mine, got)
    weight_sum = lax.psum_scatter(pair, "x", scatter_dimension=0, tiled=True)
    mixed, route_t, grads, down = pl.pallas_call(
        functools.partial(finish_kernel, hid=hid, cut=cut),
        out_shape=(
            jax.ShapeDtypeStruct((tokens, d), BF16),
            jax.ShapeDtypeStruct((per, tokens), F32),
            jax.ShapeDtypeStruct((slots, pre_width), BF16),
            jax.ShapeDtypeStruct((piece, hid), F32),
        ),
        name="finish",
    )(home, pre, rw_t, ids_t, weight_sum)
    return mixed, route_t.T, grads.reshape(tokens, per, pre_width), down[None]


def solution(mesh):
    fine = Mesh(mesh.devices.reshape(8, 2, 8, 8), ("x", "c", "y", "z"))
    every = ("x", "c", "y", "z")
    in_specs = (
        P(every, None, None),
        P(every, None),
        P(every, None),
        P(("y", "z"), None, None),
        P(every, None),
    )
    out_specs = (
        P(every, None),
        P(every, None),
        P(every, None, None),
        P(("y", "z"), ("x", "c"), None),
    )
    return jax.shard_map(
        on_device, mesh=fine, in_specs=in_specs, out_specs=out_specs, check_vma=False
    )
```
